512 devices in a mesh: shot: 16 (over z_lo, core), recv: 32 (over z_hi, y, x).
Axes of the slice: x: 4, y: 4, z: 16 (z_hi: 2, z_lo: 8; z = z_hi * 8 + z_lo), core: 2. Of those that a mesh axis runs over, the one named last changes fastest.
Arguments:
- pressure: bfloat16 [2, 6144, 6144], P(None, 'recv', 'shot'), may hold values from -6 to 6
Outputs:
- multiples: float32 [2, 6144, 6144], P(None, 'recv', 'shot')
The draws below stay inside these ranges and needn't reach their ends.
All inputs are finite; a program needn't handle non-finite values.
Results may differ from the reference program's by a relative error of at most 0.0044.
Values may be sent and summed in bfloat16 or wider, within the bound.
No kernel may reach another device: no remote copies, remote signals or barrier semaphores. Data moves between devices by JAX's collectives and lax.ppermute only.
A program may use at most 64 MiB of HBM per device.

```python
import math
import jax
import jax.numpy as jnp
from jax import lax

N = 6144


def block_scale(rng, shape, cuts, low, high):
    def one(axis_at, blocks):
        heights = jax.random.uniform(jax.random.fold_in(jax.random.fold_in(rng, 6), axis_at), (blocks,), jnp.float32, low / len(cuts), high / len(cuts))
        return jnp.repeat(jnp.exp(heights), shape[axis_at] // blocks).reshape((-1,) + (1,) * (len(shape) - axis_at - 1))

    factor_of = one(*cuts[0])
    for cut in cuts[1:]:
        factor_of = factor_of * one(*cut)
    return factor_of


def centred(key, dims, deviation, reach, shards=(), kind=jnp.bfloat16):
    factor_of = block_scale(key, dims, shards, -0.22, 0.18) if shards else 1.0
    result = jax.random.normal(key, dims, jnp.float32) * deviation * factor_of
    return jnp.minimum(jnp.maximum(result, -reach), reach).astype(kind)


def setup_inputs(seed: int = 0) -> dict:
    key_of = jax.random.split(jax.random.key(seed), 2)
    pressure = centred(key_of[0], (2, N, N), 1.0, 6.0, ((1, 32), (2, 16)))
    return {"pressure": pressure}


def reference(pressure):
    part_real = pressure[0].astype(jnp.float32)
    part_imag = pressure[1].astype(jnp.float32)
    sym_real = ((part_real + part_real.T) * 0.5).astype(jnp.bfloat16)
    sym_imag = ((part_imag + part_imag.T) * 0.5).astype(jnp.bfloat16)
    sym_real = lax.optimization_barrier(sym_real)
    sym_imag = lax.optimization_barrier(sym_imag)
    left_side = jnp.concatenate([sym_real, sym_imag], axis=1).astype(jnp.float32)
    upper_half = jnp.concatenate([sym_real, sym_imag], axis=1)
    lower_half = jnp.concatenate([-sym_imag, sym_real], axis=1)
    right_side = jnp.concatenate([upper_half, lower_half], axis=0).astype(jnp.float32)
    product = jnp.dot(left_side, right_side, precision=lax.Precision.HIGHEST, preferred_element_type=jnp.float32)
    product = product * (1.0 / math.sqrt(N))
    return jnp.stack([product[:, :N], product[:, N:]])
```

```python
import math

import jax
import jax.numpy as jnp
from jax import lax
from jax.sharding import Mesh
from jax.sharding import PartitionSpec as P

N = 6144


def mirror_pairs(n_recv, n_shot, flip):
    pairs = []
    for i in range(n_recv):
        for j in range(n_shot):
            h = (i % 2) ^ flip
            pairs.append((j * n_recv + i, (i // 2) * n_recv + 2 * j + h))
    return pairs


def local(pressure):
    n_shot = lax.axis_size("shot")
    n_half = lax.axis_size("yx")
    n_recv = 2 * n_half
    block_rows = pressure.shape[1]
    shot_index = lax.axis_index("shot")
    half_index = lax.axis_index("zh")
    recv_index = half_index * n_half + lax.axis_index("yx")
    parity = recv_index % 2
    axes = ("shot", "zh", "yx")

    arrived = []
    for flip in range(2):
        sent_half = (parity + flip) % 2
        piece = lax.dynamic_slice_in_dim(pressure, sent_half * block_rows, block_rows, 2)
        arrived.append(lax.ppermute(piece, axes, mirror_pairs(n_recv, n_shot, flip)))
    upper = jnp.where(parity == 0, arrived[0], arrived[1])
    lower = jnp.where(parity == 0, arrived[1], arrived[0])
    mirror = jnp.concatenate([upper, lower], axis=1)
    symmetric = (
        (pressure.astype(jnp.float32) + jnp.swapaxes(mirror, 1, 2).astype(jnp.float32)) * 0.5
    ).astype(jnp.bfloat16)

    partner_block = lax.ppermute(symmetric, "zh", [(0, 1), (1, 0)])
    top = jnp.where(half_index == 0, symmetric, partner_block)
    bottom = jnp.where(half_index == 0, partner_block, symmetric)
    stacked = jnp.stack([top, bottom], axis=1)
    col_panel = lax.all_gather(stacked, "yx", axis=2, tiled=False)
    col_panel = col_panel.reshape(2, n_recv * block_rows, stacked.shape[-1])

    row_panel = lax.all_gather(symmetric, "shot", axis=2, tiled=True)
    factor = 1.0 / math.sqrt(N)
    upper_half = jnp.concatenate([col_panel[0], col_panel[1]], axis=1)
    lower_half = jnp.concatenate([-col_panel[1], col_panel[0]], axis=1)
    running = jnp.dot(row_panel[0], upper_half, preferred_element_type=jnp.float32)
    running = running + jnp.dot(row_panel[1], lower_half, preferred_element_type=jnp.float32)
    running = running * factor
    block_cols = pressure.shape[2]
    return jnp.stack([running[:, :block_cols], running[:, block_cols:]])


def solution(mesh):
    n_shot, n_recv = mesh.devices.shape
    split = Mesh(mesh.devices.reshape(n_shot, 2, n_recv // 2), ("shot", "zh", "yx"))
    placed = (P(None, ("zh", "yx"), "shot"),)
    return jax.shard_map(
        local, mesh=split, in_specs=placed, out_specs=P(None, ("zh", "yx"), "shot"), check_vma=False
    )
```

```python
import math

import jax
import jax.numpy as jnp
from jax import lax
from jax.sharding import Mesh
from jax.sharding import PartitionSpec as P

N = 6144


def mirror_pairs(n_recv, n_shot, flip):
    pairs = []
    for i in range(n_recv):
        for j in range(n_shot):
            h = (i % 2) ^ flip
            pairs.append((j * n_recv + i, (i // 2) * n_recv + 2 * j + h))
    return pairs


def gather_line(block):
    n_line = lax.axis_size("zl")
    line_index = lax.axis_index("zl")
    core_index = lax.axis_index("core")
    from_left, from_right = [], []
    rightward, leftward = block, block
    for _ in range(n_line - 1):
        rightward = lax.ppermute(rightward, "zl", [(k, k + 1) for k in range(n_line - 1)])
        leftward = lax.ppermute(leftward, "zl", [(k + 1, k) for k in range(n_line - 1)])
        from_left.append(rightward)
        from_right.append(leftward)
    sequence = jnp.stack(from_left[::-1] + [block] + from_right)
    mine = lax.dynamic_slice_in_dim(sequence, n_line - 1 - line_index, n_line, 0)
    other = lax.ppermute(mine, "core", [(0, 1), (1, 0)])
    both = jnp.where(
        core_index == 0, jnp.stack([mine, other], axis=1), jnp.stack([other, mine], axis=1)
    )
    parts, rows, cols = block.shape
    return jnp.transpose(both, (2, 3, 0, 1, 4)).reshape(parts, rows, 2 * n_line * cols)


def local(pressure):
    n_shot = lax.axis_size("zl") * lax.axis_size("core")
    n_half = lax.axis_size("yx")
    n_recv = 2 * n_half
    block_rows = pressure.shape[1]
    shot_index = lax.axis_index("zl") * lax.axis_size("core") + lax.axis_index("core")
    half_index = lax.axis_index("zh")
    recv_index = half_index * n_half + lax.axis_index("yx")
    parity = recv_index % 2
    axes = ("zl", "core", "zh", "yx")

    arrived = []
    for flip in range(2):
        sent_half = (parity + flip) % 2
        piece = lax.dynamic_slice_in_dim(pressure, sent_half * block_rows, block_rows, 2)
        arrived.append(lax.ppermute(piece, axes, mirror_pairs(n_recv, n_shot, flip)))
    upper = jnp.where(parity == 0, arrived[0], arrived[1])
    lower = jnp.where(parity == 0, arrived[1], arrived[0])
    mirror = jnp.concatenate([upper, lower], axis=1)
    symmetric = (
        (pressure.astype(jnp.float32) + jnp.swapaxes(mirror, 1, 2).astype(jnp.float32)) * 0.5
    ).astype(jnp.bfloat16)

    partner_block = lax.ppermute(symmetric, "zh", [(0, 1), (1, 0)])
    top = jnp.where(half_index == 0, symmetric, partner_block)
    bottom = jnp.where(half_index == 0, partner_block, symmetric)
    stacked = jnp.stack([top, bottom], axis=1)
    col_panel = lax.all_gather(stacked, "yx", axis=2, tiled=False)
    col_panel = col_panel.reshape(2, n_recv * block_rows, stacked.shape[-1])

    row_panel = gather_line(symmetric)
    factor = 1.0 / math.sqrt(N)
    upper_half = jnp.concatenate([col_panel[0], col_panel[1]], axis=1)
    lower_half = jnp.concatenate([-col_panel[1], col_panel[0]], axis=1)
    running = jnp.dot(row_panel[0], upper_half, preferred_element_type=jnp.float32)
    running = running + jnp.dot(row_panel[1], lower_half, preferred_element_type=jnp.float32)
    running = running * factor
    block_cols = pressure.shape[2]
    return jnp.stack([running[:, :block_cols], running[:, block_cols:]])


def solution(mesh):
    n_shot, n_recv = mesh.devices.shape
    split = Mesh(
        mesh.devices.reshape(n_shot // 2, 2, 2, n_recv // 2), ("zl", "core", "zh", "yx")
    )
    placed = P(None, ("zh", "yx"), ("zl", "core"))
    return jax.shard_map(local, mesh=split, in_specs=(placed,), out_specs=placed, check_vma=False)
```

```python
import math

import jax
import jax.numpy as jnp
from jax import lax
from jax.sharding import Mesh
from jax.sharding import PartitionSpec as P

N = 6144


def mirror_pairs(n_recv, n_shot, flip):
    pairs = []
    for i in range(n_recv):
        for j in range(n_shot):
            h = (i % 2) ^ flip
            pairs.append((j * n_recv + i, (i // 2) * n_recv + 2 * j + h))
    return pairs


def gather_line(block):
    n_line = lax.axis_size("zl")
    line_index = lax.axis_index("zl")
    core_index = lax.axis_index("core")
    from_left, from_right = [], []
    rightward, leftward = block, block
    for _ in range(n_line - 1):
        rightward = lax.ppermute(rightward, "zl", [(k, k + 1) for k in range(n_line - 1)])
        leftward = lax.ppermute(leftward, "zl", [(k + 1, k) for k in range(n_line - 1)])
        from_left.append(rightward)
        from_right.append(leftward)
    sequence = jnp.stack(from_left[::-1] + [block] + from_right)
    mine = lax.dynamic_slice_in_dim(sequence, n_line - 1 - line_index, n_line, 0)
    other = lax.ppermute(mine, "core", [(0, 1), (1, 0)])
    both = jnp.where(
        core_index == 0, jnp.stack([mine, other], axis=1), jnp.stack([other, mine], axis=1)
    )
    return both.reshape((2 * n_line,) + block.shape)


def local(pressure):
    n_shot = lax.axis_size("zl") * lax.axis_size("core")
    n_half = lax.axis_size("yx")
    n_recv = 2 * n_half
    block_rows = pressure.shape[1]
    shot_index = lax.axis_index("zl") * lax.axis_size("core") + lax.axis_index("core")
    half_index = lax.axis_index("zh")
    recv_index = half_index * n_half + lax.axis_index("yx")
    parity = recv_index % 2
    axes = ("zl", "core", "zh", "yx")

    arrived = []
    for flip in range(2):
        sent_half = (parity + flip) % 2
        piece = lax.dynamic_slice_in_dim(pressure, sent_half * block_rows, block_rows, 2)
        arrived.append(lax.ppermute(piece, axes, mirror_pairs(n_recv, n_shot, flip)))
    upper = jnp.where(parity == 0, arrived[0], arrived[1])
    lower = jnp.where(parity == 0, arrived[1], arrived[0])
    mirror = jnp.concatenate([upper, lower], axis=1)
    symmetric = (
        (pressure.astype(jnp.float32) + jnp.swapaxes(mirror, 1, 2).astype(jnp.float32)) * 0.5
    ).astype(jnp.bfloat16)

    partner_block = lax.ppermute(symmetric, "zh", [(0, 1), (1, 0)])
    own_panel = lax.all_gather(symmetric, "yx", axis=0, tiled=False)
    partner_panel = lax.all_gather(partner_block, "yx", axis=0, tiled=False)
    row_blocks = gather_line(symmetric)

    n_blocks = row_blocks.shape[0]
    parts, rows, cols = symmetric.shape
    row_blocks = row_blocks.reshape(n_blocks, parts, rows, 2, cols // 2)
    own_rows = lax.dynamic_slice_in_dim(row_blocks, half_index * (n_blocks // 2), n_blocks // 2, 0)
    other_rows = lax.dynamic_slice_in_dim(
        row_blocks, (1 - half_index) * (n_blocks // 2), n_blocks // 2, 0
    )

    def product(left, panel):
        panel = panel.reshape(n_blocks // 2, 2, parts, rows, cols)
        return jnp.einsum("jpxhr,jhqrn->pqxn", left, panel, preferred_element_type=jnp.float32)

    terms = product(own_rows, own_panel) + product(other_rows, partner_panel)
    factor = 1.0 / math.sqrt(N)
    real = (terms[0, 0] - terms[1, 1]) * factor
    imag = (terms[0, 1] + terms[1, 0]) * factor
    return jnp.stack([real, imag])


def solution(mesh):
    n_shot, n_recv = mesh.devices.shape
    split = Mesh(
        mesh.devices.reshape(n_shot // 2, 2, 2, n_recv // 2), ("zl", "core", "zh", "yx")
    )
    placed = P(None, ("zh", "yx"), ("zl", "core"))
    return jax.shard_map(local, mesh=split, in_specs=(placed,), out_specs=placed, check_vma=False)
```

```python
import math

import jax
import jax.numpy as jnp
from jax import lax
from jax.sharding import Mesh
from jax.sharding import PartitionSpec as P

N = 6144


def mirror_pairs(n_recv, n_shot, flip):
    pairs = []
    for i in range(n_recv):
        for j in range(n_shot):
            h = (i % 2) ^ flip
            pairs.append((j * n_recv + i, (i // 2) * n_recv + 2 * j + h))
    return pairs


def gather_line(block):
    n_line = lax.axis_size("zl")
    line_index = lax.axis_index("zl")
    from_left, from_right = [], []
    rightward, leftward = block, block
    for _ in range(n_line - 1):
        rightward = lax.ppermute(rightward, "zl", [(k, k + 1) for k in range(n_line - 1)])
        leftward = lax.ppermute(leftward, "zl", [(k + 1, k) for k in range(n_line - 1)])
        from_left.append(rightward)
        from_right.append(leftward)
    sequence = jnp.stack(from_left[::-1] + [block] + from_right)
    mine = lax.dynamic_slice_in_dim(sequence, n_line - 1 - line_index, n_line, 0)
    other = lax.ppermute(mine, "core", [(0, 1), (1, 0)])
    return mine, other


def gather_plane(block):
    n_y = lax.axis_size("y")
    n_x = lax.axis_size("x")
    rows = []
    for dy in range(n_y):
        row = []
        for dx in range(n_x):
            if dy == 0 and dx == 0:
                row.append(block)
                continue
            pairs = [
                (y * n_x + x, ((y - dy) % n_y) * n_x + (x - dx) % n_x)
                for y in range(n_y)
                for x in range(n_x)
            ]
            row.append(lax.ppermute(block, ("y", "x"), pairs))
        rows.append(jnp.stack(row))
    relative = jnp.stack(rows)
    placed = jnp.roll(relative, (lax.axis_index("y"), lax.axis_index("x")), axis=(0, 1))
    return placed.reshape((n_y * n_x,) + block.shape)


def local(pressure):
    n_shot = lax.axis_size("zl") * lax.axis_size("core")
    n_half = lax.axis_size("y") * lax.axis_size("x")
    n_recv = 2 * n_half
    block_rows = pressure.shape[1]
    shot_index = lax.axis_index("zl") * lax.axis_size("core") + lax.axis_index("core")
    half_index = lax.axis_index("zh")
    recv_index = half_index * n_half + lax.axis_index("y") * lax.axis_size("x") + lax.axis_index("x")
    parity = recv_index % 2
    axes = ("zl", "core", "zh", "y", "x")

    arrived = []
    for flip in range(2):
        sent_half = (parity + flip) % 2
        piece = lax.dynamic_slice_in_dim(pressure, sent_half * block_rows, block_rows, 2)
        arrived.append(lax.ppermute(piece, axes, mirror_pairs(n_recv, n_shot, flip)))
    upper = jnp.where(parity == 0, arrived[0], arrived[1])
    lower = jnp.where(parity == 0, arrived[1], arrived[0])
    mirror = jnp.concatenate([upper, lower], axis=1)
    symmetric = (
        (pressure.astype(jnp.float32) + jnp.swapaxes(mirror, 1, 2).astype(jnp.float32)) * 0.5
    ).astype(jnp.bfloat16)

    partner_block = lax.ppermute(symmetric, "zh", [(0, 1), (1, 0)])
    own_panel = gather_plane(symmetric)
    partner_panel = gather_plane(partner_block)
    mine, other = gather_line(symmetric)
    core_index = lax.axis_index("core")
    n_line = mine.shape[0]
    parts, rows, cols = symmetric.shape

    def product(left, panel, parity):
        panel = panel.reshape(n_line // 2, 2, 2, parts, rows, cols)
        panel = lax.dynamic_index_in_dim(panel, parity, 1, keepdims=False)
        panel = jnp.swapaxes(panel, 1, 2).reshape(n_line // 2, parts, 2 * rows, cols)
        return jnp.einsum("zpxc,zqcn->pqxn", left, panel, preferred_element_type=jnp.float32)

    quarter = n_line // 2
    own_start = half_index * quarter
    other_start = (1 - half_index) * quarter
    terms = (
        product(lax.dynamic_slice_in_dim(mine, own_start, quarter, 0), own_panel, core_index)
        + product(lax.dynamic_slice_in_dim(other, own_start, quarter, 0), own_panel, 1 - core_index)
        + product(lax.dynamic_slice_in_dim(mine, other_start, quarter, 0), partner_panel, core_index)
        + product(lax.dynamic_slice_in_dim(other, other_start, quarter, 0), partner_panel, 1 - core_index)
    )
    factor = 1.0 / math.sqrt(N)
    real = (terms[0, 0] - terms[1, 1]) * factor
    imag = (terms[0, 1] + terms[1, 0]) * factor
    return jnp.stack([real, imag])


def solution(mesh):
    n_shot, n_recv = mesh.devices.shape
    n_x = 4
    split = Mesh(
        mesh.devices.reshape(n_shot // 2, 2, 2, n_recv // (2 * n_x), n_x),
        ("zl", "core", "zh", "y", "x"),
    )
    placed = P(None, ("zh", "y", "x"), ("zl", "core"))
    return jax.shard_map(local, mesh=split, in_specs=(placed,), out_specs=placed, check_vma=False)
```

```python
import math

import jax
import jax.numpy as jnp
from jax import lax
from jax.sharding import Mesh
from jax.sharding import PartitionSpec as P

N = 6144


def mirror_pairs(n_recv, n_shot, flip):
    pairs = []
    for i in range(n_recv):
        for j in range(n_shot):
            h = (i % 2) ^ flip
            pairs.append((j * n_recv + i, (i // 2) * n_recv + 2 * j + h))
    return pairs


def gather_line(block):
    n_line = lax.axis_size("zl")
    line_index = lax.axis_index("zl")
    from_left, from_right = [], []
    rightward, leftward = block, block
    for _ in range(n_line - 1):
        rightward = lax.ppermute(rightward, "zl", [(k, k + 1) for k in range(n_line - 1)])
        leftward = lax.ppermute(leftward, "zl", [(k + 1, k) for k in range(n_line - 1)])
        from_left.append(rightward)
        from_right.append(leftward)
    sequence = jnp.stack(from_left[::-1] + [block] + from_right)
    mine = lax.dynamic_slice_in_dim(sequence, n_line - 1 - line_index, n_line, 0)
    other = lax.ppermute(mine, "core", [(0, 1), (1, 0)])
    return mine, other


def local(pressure):
    n_shot = lax.axis_size("zl") * lax.axis_size("core")
    n_half = lax.axis_size("y") * lax.axis_size("x")
    n_recv = 2 * n_half
    block_rows = pressure.shape[1]
    shot_index = lax.axis_index("zl") * lax.axis_size("core") + lax.axis_index("core")
    half_index = lax.axis_index("zh")
    recv_index = half_index * n_half + lax.axis_index("y") * lax.axis_size("x") + lax.axis_index("x")
    parity = recv_index % 2
    axes = ("zl", "core", "zh", "y", "x")

    arrived = []
    for flip in range(2):
        sent_half = (parity + flip) % 2
        piece = lax.dynamic_slice_in_dim(pressure, sent_half * block_rows, block_rows, 2)
        arrived.append(lax.ppermute(piece, axes, mirror_pairs(n_recv, n_shot, flip)))
    upper = jnp.where(parity == 0, arrived[0], arrived[1])
    lower = jnp.where(parity == 0, arrived[1], arrived[0])
    mirror = jnp.concatenate([upper, lower], axis=1)
    symmetric = (
        (pressure.astype(jnp.float32) + jnp.swapaxes(mirror, 1, 2).astype(jnp.float32)) * 0.5
    ).astype(jnp.bfloat16)

    partner_block = lax.ppermute(symmetric, "zh", [(0, 1), (1, 0)])
    top = jnp.where(half_index == 0, symmetric, partner_block)
    bottom = jnp.where(half_index == 0, partner_block, symmetric)
    panels = lax.all_gather(jnp.stack([top, bottom]), ("y", "x"), axis=1, tiled=False)
    mine, other = gather_line(symmetric)
    core_index = lax.axis_index("core")
    n_line = mine.shape[0]
    parts, rows, cols = symmetric.shape

    def product(left, panel, parity):
        panel = panel.reshape(n_line // 2, 2, 2, parts, rows, cols)
        panel = lax.dynamic_index_in_dim(panel, parity, 1, keepdims=False)
        panel = jnp.swapaxes(panel, 1, 2).reshape(n_line // 2, parts, 2 * rows, cols)
        return jnp.einsum("zpxc,zqcn->pqxn", left, panel, preferred_element_type=jnp.float32)

    quarter = n_line // 2
    terms = (
        product(mine[:quarter], panels[0], core_index)
        + product(other[:quarter], panels[0], 1 - core_index)
        + product(mine[quarter:], panels[1], core_index)
        + product(other[quarter:], panels[1], 1 - core_index)
    )
    factor = 1.0 / math.sqrt(N)
    real = (terms[0, 0] - terms[1, 1]) * factor
    imag = (terms[0, 1] + terms[1, 0]) * factor
    return jnp.stack([real, imag])


def solution(mesh):
    n_shot, n_recv = mesh.devices.shape
    n_x = 4
    split = Mesh(
        mesh.devices.reshape(n_shot // 2, 2, 2, n_recv // (2 * n_x), n_x),
        ("zl", "core", "zh", "y", "x"),
    )
    placed = P(None, ("zh", "y", "x"), ("zl", "core"))
    return jax.shard_map(local, mesh=split, in_specs=(placed,), out_specs=placed, check_vma=False)
```

```python
import math

import jax
import jax.numpy as jnp
from jax import lax
from jax.sharding import Mesh
from jax.sharding import PartitionSpec as P

N = 6144


def mirror_pairs(n_recv, n_shot, flip):
    pairs = []
    for i in range(n_recv):
        for j in range(n_shot):
            h = (i % 2) ^ flip
            pairs.append((j * n_recv + i, (i // 2) * n_recv + 2 * j + h))
    return pairs


def gather_line(block):
    n_line = lax.axis_size("zl")
    line_index = lax.axis_index("zl")
    from_left, from_right = [], []
    rightward, leftward = block, block
    for _ in range(n_line - 1):
        rightward = lax.ppermute(rightward, "zl", [(k, k + 1) for k in range(n_line - 1)])
        leftward = lax.ppermute(leftward, "zl", [(k + 1, k) for k in range(n_line - 1)])
        from_left.append(rightward)
        from_right.append(leftward)
    sequence = jnp.stack(from_left[::-1] + [block] + from_right)
    mine = lax.dynamic_slice_in_dim(sequence, n_line - 1 - line_index, n_line, 0)
    other = lax.ppermute(mine, "core", [(0, 1), (1, 0)])
    return mine, other


def local(pressure):
    n_shot = lax.axis_size("zl") * lax.axis_size("core")
    n_half = lax.axis_size("y") * lax.axis_size("x")
    n_recv = 2 * n_half
    block_rows = pressure.shape[1]
    shot_index = lax.axis_index("zl") * lax.axis_size("core") + lax.axis_index("core")
    half_index = lax.axis_index("zh")
    recv_index = half_index * n_half + lax.axis_index("y") * lax.axis_size("x") + lax.axis_index("x")
    parity = recv_index % 2
    axes = ("zl", "core", "zh", "y", "x")

    arrived = []
    for flip in range(2):
        sent_half = (parity + flip) % 2
        piece = lax.dynamic_slice_in_dim(pressure, sent_half * block_rows, block_rows, 2)
        arrived.append(lax.ppermute(piece, axes, mirror_pairs(n_recv, n_shot, flip)))
    upper = jnp.where(parity == 0, arrived[0], arrived[1])
    lower = jnp.where(parity == 0, arrived[1], arrived[0])
    mirror = jnp.concatenate([upper, lower], axis=1)
    symmetric = (
        (pressure.astype(jnp.float32) + jnp.swapaxes(mirror, 1, 2).astype(jnp.float32)) * 0.5
    ).astype(jnp.bfloat16)

    partner_block = lax.ppermute(symmetric, "zh", [(0, 1), (1, 0)])
    top = jnp.where(half_index == 0, symmetric, partner_block)
    bottom = jnp.where(half_index == 0, partner_block, symmetric)
    panels = lax.all_gather(jnp.stack([top, bottom]), "x", axis=1, tiled=False)
    panels = lax.all_gather(panels, "y", axis=1, tiled=False)
    panels = panels.reshape((2, -1) + symmetric.shape)
    mine, other = gather_line(symmetric)
    core_index = lax.axis_index("core")
    n_line = mine.shape[0]
    parts, rows, cols = symmetric.shape

    def product(left, panel, parity):
        panel = panel.reshape(n_line // 2, 2, 2, parts, rows, cols)
        panel = lax.dynamic_index_in_dim(panel, parity, 1, keepdims=False)
        panel = jnp.swapaxes(panel, 1, 2).reshape(n_line // 2, parts, 2 * rows, cols)
        return jnp.einsum("zpxc,zqcn->pqxn", left, panel, preferred_element_type=jnp.float32)

    quarter = n_line // 2
    terms = (
        product(mine[:quarter], panels[0], core_index)
        + product(other[:quarter], panels[0], 1 - core_index)
        + product(mine[quarter:], panels[1], core_index)
        + product(other[quarter:], panels[1], 1 - core_index)
    )
    factor = 1.0 / math.sqrt(N)
    real = (terms[0, 0] - terms[1, 1]) * factor
    imag = (terms[0, 1] + terms[1, 0]) * factor
    return jnp.stack([real, imag])


def solution(mesh):
    n_shot, n_recv = mesh.devices.shape
    n_x = 4
    split = Mesh(
        mesh.devices.reshape(n_shot // 2, 2, 2, n_recv // (2 * n_x), n_x),
        ("zl", "core", "zh", "y", "x"),
    )
    placed = P(None, ("zh", "y", "x"), ("zl", "core"))
    return jax.shard_map(local, mesh=split, in_specs=(placed,), out_specs=placed, check_vma=False)
```

```python
import math

import jax
import jax.numpy as jnp
from jax import lax
from jax.sharding import Mesh
from jax.sharding import PartitionSpec as P

N = 6144


def mirror_pairs(n_recv, n_shot, flip):
    pairs = []
    for i in range(n_recv):
        for j in range(n_shot):
            h = (i % 2) ^ flip
            pairs.append((j * n_recv + i, (i // 2) * n_recv + 2 * j + h))
    return pairs


def gather_line(block):
    n_line = lax.axis_size("zl")
    line_index = lax.axis_index("zl")
    from_left, from_right = [], []
    rightward, leftward = block, block
    for _ in range(n_line - 1):
        rightward = lax.ppermute(rightward, "zl", [(k, k + 1) for k in range(n_line - 1)])
        leftward = lax.ppermute(leftward, "zl", [(k + 1, k) for k in range(n_line - 1)])
        from_left.append(rightward)
        from_right.append(leftward)
    sequence = jnp.stack(from_left[::-1] + [block] + from_right)
    mine = lax.dynamic_slice_in_dim(sequence, n_line - 1 - line_index, n_line, 0)
    other = lax.ppermute(mine, "core", [(0, 1), (1, 0)])
    return mine, other


def ring_shift(value, shift):
    n_line = lax.axis_size("zl")
    n_ring = 2 * n_line
    pairs = []
    for line in range(n_line):
        for half in range(2):
            target = (half * n_line + line + shift) % n_ring
            pairs.append((line * 2 + half, (target % n_line) * 2 + target // n_line))
    return lax.ppermute(value, ("zl", "zh"), pairs)


def cross_halves(block):
    quarter = lax.axis_size("zl") // 2
    forward = ring_shift(ring_shift(block[0], quarter), quarter)
    backward = ring_shift(ring_shift(block[1], -quarter), -quarter)
    return jnp.stack([forward, backward])


def local(pressure):
    n_shot = lax.axis_size("zl") * lax.axis_size("core")
    n_half = lax.axis_size("y") * lax.axis_size("x")
    n_recv = 2 * n_half
    block_rows = pressure.shape[1]
    shot_index = lax.axis_index("zl") * lax.axis_size("core") + lax.axis_index("core")
    half_index = lax.axis_index("zh")
    recv_index = half_index * n_half + lax.axis_index("y") * lax.axis_size("x") + lax.axis_index("x")
    parity = recv_index % 2
    axes = ("zl", "core", "zh", "y", "x")

    arrived = []
    for flip in range(2):
        sent_half = (parity + flip) % 2
        piece = lax.dynamic_slice_in_dim(pressure, sent_half * block_rows, block_rows, 2)
        arrived.append(lax.ppermute(piece, axes, mirror_pairs(n_recv, n_shot, flip)))
    upper = jnp.where(parity == 0, arrived[0], arrived[1])
    lower = jnp.where(parity == 0, arrived[1], arrived[0])
    mirror = jnp.concatenate([upper, lower], axis=1)
    symmetric = (
        (pressure.astype(jnp.float32) + jnp.swapaxes(mirror, 1, 2).astype(jnp.float32)) * 0.5
    ).astype(jnp.bfloat16)

    partner_block = cross_halves(symmetric)
    top = jnp.where(half_index == 0, symmetric, partner_block)
    bottom = jnp.where(half_index == 0, partner_block, symmetric)
    panels = lax.all_gather(jnp.stack([top, bottom]), ("y", "x"), axis=1, tiled=False)
    mine, other = gather_line(symmetric)
    core_index = lax.axis_index("core")
    n_line = mine.shape[0]
    parts, rows, cols = symmetric.shape

    def product(left, panel, parity):
        panel = panel.reshape(n_line // 2, 2, 2, parts, rows, cols)
        panel = lax.dynamic_index_in_dim(panel, parity, 1, keepdims=False)
        panel = jnp.swapaxes(panel, 1, 2).reshape(n_line // 2, parts, 2 * rows, cols)
        return jnp.einsum("zpxc,zqcn->pqxn", left, panel, preferred_element_type=jnp.float32)

    quarter = n_line // 2
    terms = (
        product(mine[:quarter], panels[0], core_index)
        + product(other[:quarter], panels[0], 1 - core_index)
        + product(mine[quarter:], panels[1], core_index)
        + product(other[quarter:], panels[1], 1 - core_index)
    )
    factor = 1.0 / math.sqrt(N)
    real = (terms[0, 0] - terms[1, 1]) * factor
    imag = (terms[0, 1] + terms[1, 0]) * factor
    return jnp.stack([real, imag])


def solution(mesh):
    n_shot, n_recv = mesh.devices.shape
    n_x = 4
    split = Mesh(
        mesh.devices.reshape(n_shot // 2, 2, 2, n_recv // (2 * n_x), n_x),
        ("zl", "core", "zh", "y", "x"),
    )
    placed = P(None, ("zh", "y", "x"), ("zl", "core"))
    return jax.shard_map(local, mesh=split, in_specs=(placed,), out_specs=placed, check_vma=False)
```

```python
import math

import jax
import jax.numpy as jnp
from jax import lax
from jax.sharding import Mesh
from jax.sharding import PartitionSpec as P

N = 6144


def mirror_pairs(n_recv, n_shot, flip, across):
    pairs = []
    for i in range(n_recv):
        for j in range(n_shot):
            h = (i % 2) ^ flip
            target = (2 * j + h + across * n_recv // 2) % n_recv
            pairs.append((j * n_recv + i, (i // 2) * n_recv + target))
    return pairs


def gather_line(block):
    n_line = lax.axis_size("zl")
    line_index = lax.axis_index("zl")
    from_left, from_right = [], []
    rightward, leftward = block, block
    for _ in range(n_line - 1):
        rightward = lax.ppermute(rightward, "zl", [(k, k + 1) for k in range(n_line - 1)])
        leftward = lax.ppermute(leftward, "zl", [(k + 1, k) for k in range(n_line - 1)])
        from_left.append(rightward)
        from_right.append(leftward)
    sequence = jnp.stack(from_left[::-1] + [block] + from_right)
    mine = lax.dynamic_slice_in_dim(sequence, n_line - 1 - line_index, n_line, 0)
    other = lax.ppermute(mine, "core", [(0, 1), (1, 0)])
    return mine, other


def local(pressure):
    n_shot = lax.axis_size("zl") * lax.axis_size("core")
    n_half = lax.axis_size("y") * lax.axis_size("x")
    n_recv = 2 * n_half
    block_rows = pressure.shape[1]
    shot_index = lax.axis_index("zl") * lax.axis_size("core") + lax.axis_index("core")
    half_index = lax.axis_index("zh")
    recv_index = half_index * n_half + lax.axis_index("y") * lax.axis_size("x") + lax.axis_index("x")
    parity = recv_index % 2
    axes = ("zl", "core", "zh", "y", "x")

    partner_raw = lax.ppermute(pressure, "zh", [(0, 1), (1, 0)])

    def symmetrize(raw, across):
        arrived = []
        for flip in range(2):
            sent_half = (parity + flip) % 2
            piece = lax.dynamic_slice_in_dim(pressure, sent_half * block_rows, block_rows, 2)
            arrived.append(lax.ppermute(piece, axes, mirror_pairs(n_recv, n_shot, flip, across)))
        upper = jnp.where(parity == 0, arrived[0], arrived[1])
        lower = jnp.where(parity == 0, arrived[1], arrived[0])
        mirror = jnp.concatenate([upper, lower], axis=1)
        return (
            (raw.astype(jnp.float32) + jnp.swapaxes(mirror, 1, 2).astype(jnp.float32)) * 0.5
        ).astype(jnp.bfloat16)

    symmetric = symmetrize(pressure, 0)
    partner_block = symmetrize(partner_raw, 1)
    top = jnp.where(half_index == 0, symmetric, partner_block)
    bottom = jnp.where(half_index == 0, partner_block, symmetric)
    panels = lax.all_gather(jnp.stack([top, bottom]), ("y", "x"), axis=1, tiled=False)
    mine, other = gather_line(symmetric)
    core_index = lax.axis_index("core")
    n_line = mine.shape[0]
    parts, rows, cols = symmetric.shape

    def product(left, panel, parity):
        panel = panel.reshape(n_line // 2, 2, 2, parts, rows, cols)
        panel = lax.dynamic_index_in_dim(panel, parity, 1, keepdims=False)
        panel = jnp.swapaxes(panel, 1, 2).reshape(n_line // 2, parts, 2 * rows, cols)
        return jnp.einsum("zpxc,zqcn->pqxn", left, panel, preferred_element_type=jnp.float32)

    quarter = n_line // 2
    terms = (
        product(mine[:quarter], panels[0], core_index)
        + product(other[:quarter], panels[0], 1 - core_index)
        + product(mine[quarter:], panels[1], core_index)
        + product(other[quarter:], panels[1], 1 - core_index)
    )
    factor = 1.0 / math.sqrt(N)
    real = (terms[0, 0] - terms[1, 1]) * factor
    imag = (terms[0, 1] + terms[1, 0]) * factor
    return jnp.stack([real, imag])


def solution(mesh):
    n_shot, n_recv = mesh.devices.shape
    n_x = 4
    split = Mesh(
        mesh.devices.reshape(n_shot // 2, 2, 2, n_recv // (2 * n_x), n_x),
        ("zl", "core", "zh", "y", "x"),
    )
    placed = P(None, ("zh", "y", "x"), ("zl", "core"))
    return jax.shard_map(local, mesh=split, in_specs=(placed,), out_specs=placed, check_vma=False)
```

```python
import math

import jax
import jax.numpy as jnp
from jax import lax
from jax.sharding import Mesh
from jax.sharding import PartitionSpec as P

N = 6144


def mirror_pairs(n_recv, n_shot, flip):
    pairs = []
    for i in range(n_recv):
        for j in range(n_shot):
            h = (i % 2) ^ flip
            pairs.append((j * n_recv + i, (i // 2) * n_recv + 2 * j + h))
    return pairs


def gather_line(block):
    n_line = lax.axis_size("zl")
    line_index = lax.axis_index("zl")
    from_left, from_right = [], []
    rightward, leftward = block, block
    for _ in range(n_line - 1):
        rightward = lax.ppermute(rightward, "zl", [(k, k + 1) for k in range(n_line - 1)])
        leftward = lax.ppermute(leftward, "zl", [(k + 1, k) for k in range(n_line - 1)])
        from_left.append(rightward)
        from_right.append(leftward)
    sequence = jnp.stack(from_left[::-1] + [block] + from_right)
    mine = lax.dynamic_slice_in_dim(sequence, n_line - 1 - line_index, n_line, 0)
    other = lax.ppermute(mine, "core", [(0, 1), (1, 0)])
    return mine, other


def local(pressure):
    n_shot = lax.axis_size("zl") * lax.axis_size("core")
    n_half = lax.axis_size("y") * lax.axis_size("x")
    n_recv = 2 * n_half
    block_rows = pressure.shape[1]
    shot_index = lax.axis_index("zl") * lax.axis_size("core") + lax.axis_index("core")
    half_index = lax.axis_index("zh")
    recv_index = half_index * n_half + lax.axis_index("y") * lax.axis_size("x") + lax.axis_index("x")
    parity = recv_index % 2
    axes = ("zl", "core", "zh", "y", "x")

    arrived = []
    for flip in range(2):
        sent_half = (parity + flip) % 2
        piece = lax.dynamic_slice_in_dim(pressure, sent_half * block_rows, block_rows, 2)
        arrived.append(lax.ppermute(piece, axes, mirror_pairs(n_recv, n_shot, flip)))
    upper = jnp.where(parity == 0, arrived[0], arrived[1])
    lower = jnp.where(parity == 0, arrived[1], arrived[0])
    mirror = jnp.concatenate([upper, lower], axis=1)
    symmetric = (
        (pressure.astype(jnp.float32) + jnp.swapaxes(mirror, 1, 2).astype(jnp.float32)) * 0.5
    ).astype(jnp.bfloat16)

    partner_block = lax.ppermute(symmetric, "zh", [(0, 1), (1, 0)])
    top = jnp.where(half_index == 0, symmetric, partner_block)
    bottom = jnp.where(half_index == 0, partner_block, symmetric)
    pieces = jnp.swapaxes(jnp.stack([top, bottom]), 1, 2)
    panels = lax.all_gather(pieces, ("y", "x"), axis=1, tiled=False)
    mine, other = gather_line(symmetric)
    core_index = lax.axis_index("core")
    n_line = mine.shape[0]
    parts, rows, cols = symmetric.shape
    natural = jnp.where(
        core_index == 0, jnp.stack([mine, other], axis=1), jnp.stack([other, mine], axis=1)
    ).reshape((2 * n_line,) + symmetric.shape)

    def product(left, panel):
        panel = panel.reshape(n_line, 2 * rows, parts, cols)
        return jnp.einsum("jpxc,jcqn->pqxn", left, panel, preferred_element_type=jnp.float32)

    terms = product(natural[:n_line], panels[0]) + product(natural[n_line:], panels[1])
    factor = 1.0 / math.sqrt(N)
    real = (terms[0, 0] - terms[1, 1]) * factor
    imag = (terms[0, 1] + terms[1, 0]) * factor
    return jnp.stack([real, imag])


def solution(mesh):
    n_shot, n_recv = mesh.devices.shape
    n_x = 4
    split = Mesh(
        mesh.devices.reshape(n_shot // 2, 2, 2, n_recv // (2 * n_x), n_x),
        ("zl", "core", "zh", "y", "x"),
    )
    placed = P(None, ("zh", "y", "x"), ("zl", "core"))
    return jax.shard_map(local, mesh=split, in_specs=(placed,), out_specs=placed, check_vma=False)
```

```python
import math

import jax
import jax.numpy as jnp
from jax import lax
from jax.sharding import Mesh
from jax.sharding import PartitionSpec as P

N = 6144


def mirror_pairs(n_recv, n_shot, flip, across=0):
    pairs = []
    n_half = n_recv // 2
    for i in range(n_recv):
        for j in range(n_shot):
            h = (i % 2) ^ flip
            target = (2 * j + h + across * n_half) % n_recv
            if across and target // n_half != i // n_half:
                continue
            pairs.append((j * n_recv + i, (i // 2) * n_recv + target))
    return pairs


def gather_line(block):
    n_line = lax.axis_size("zl")
    line_index = lax.axis_index("zl")
    from_left, from_right = [], []
    rightward, leftward = block, block
    for _ in range(n_line - 1):
        rightward = lax.ppermute(rightward, "zl", [(k, k + 1) for k in range(n_line - 1)])
        leftward = lax.ppermute(leftward, "zl", [(k + 1, k) for k in range(n_line - 1)])
        from_left.append(rightward)
        from_right.append(leftward)
    sequence = jnp.stack(from_left[::-1] + [block] + from_right)
    mine = lax.dynamic_slice_in_dim(sequence, n_line - 1 - line_index, n_line, 0)
    other = lax.ppermute(mine, "core", [(0, 1), (1, 0)])
    return mine, other


def local(pressure):
    n_shot = lax.axis_size("zl") * lax.axis_size("core")
    n_half = lax.axis_size("y") * lax.axis_size("x")
    n_recv = 2 * n_half
    block_rows = pressure.shape[1]
    shot_index = lax.axis_index("zl") * lax.axis_size("core") + lax.axis_index("core")
    half_index = lax.axis_index("zh")
    recv_index = half_index * n_half + lax.axis_index("y") * lax.axis_size("x") + lax.axis_index("x")
    parity = recv_index % 2
    axes = ("zl", "core", "zh", "y", "x")

    arrived = []
    for flip in range(2):
        sent_half = (parity + flip) % 2
        piece = lax.dynamic_slice_in_dim(pressure, sent_half * block_rows, block_rows, 2)
        arrived.append(lax.ppermute(piece, axes, mirror_pairs(n_recv, n_shot, flip)))
    upper = jnp.where(parity == 0, arrived[0], arrived[1])
    lower = jnp.where(parity == 0, arrived[1], arrived[0])
    mirror = jnp.concatenate([upper, lower], axis=1)
    symmetric = (
        (pressure.astype(jnp.float32) + jnp.swapaxes(mirror, 1, 2).astype(jnp.float32)) * 0.5
    ).astype(jnp.bfloat16)

    arrived = []
    for flip in range(2):
        sent_half = (parity + flip) % 2
        piece = lax.dynamic_slice_in_dim(symmetric, sent_half * block_rows, block_rows, 2)
        arrived.append(lax.ppermute(piece, axes, mirror_pairs(n_recv, n_shot, flip, 1)))
    upper = jnp.where(parity == 0, arrived[0], arrived[1])
    lower = jnp.where(parity == 0, arrived[1], arrived[0])
    transposed = jnp.swapaxes(jnp.concatenate([upper, lower], axis=1), 1, 2)
    shot_half = n_shot // 2
    crossing = [
        (j * 2 + half, j * 2 + 1 - half)
        for j in range(n_shot)
        for half in range(2)
        if j // shot_half == half
    ]
    crossed = lax.ppermute(symmetric, ("zl", "core", "zh"), crossing)
    partner_block = jnp.where(shot_index // shot_half == half_index, transposed, crossed)
    top = jnp.where(half_index == 0, symmetric, partner_block)
    bottom = jnp.where(half_index == 0, partner_block, symmetric)
    pieces = jnp.swapaxes(jnp.stack([top, bottom]), 1, 2)
    panels = lax.all_gather(pieces, ("y", "x"), axis=1, tiled=False)
    mine, other = gather_line(symmetric)
    core_index = lax.axis_index("core")
    n_line = mine.shape[0]
    parts, rows, cols = symmetric.shape
    natural = jnp.where(
        core_index == 0, jnp.stack([mine, other], axis=1), jnp.stack([other, mine], axis=1)
    ).reshape((2 * n_line,) + symmetric.shape)

    def product(left, panel):
        panel = panel.reshape(n_line, 2 * rows, parts, cols)
        return jnp.einsum("jpxc,jcqn->pqxn", left, panel, preferred_element_type=jnp.float32)

    terms = product(natural[:n_line], panels[0]) + product(natural[n_line:], panels[1])
    factor = 1.0 / math.sqrt(N)
    real = (terms[0, 0] - terms[1, 1]) * factor
    imag = (terms[0, 1] + terms[1, 0]) * factor
    return jnp.stack([real, imag])


def solution(mesh):
    n_shot, n_recv = mesh.devices.shape
    n_x = 4
    split = Mesh(
        mesh.devices.reshape(n_shot // 2, 2, 2, n_recv // (2 * n_x), n_x),
        ("zl", "core", "zh", "y", "x"),
    )
    placed = P(None, ("zh", "y", "x"), ("zl", "core"))
    return jax.shard_map(local, mesh=split, in_specs=(placed,), out_specs=placed, check_vma=False)
```

```python
import math

import jax
import jax.numpy as jnp
from jax import lax
from jax.sharding import Mesh
from jax.sharding import PartitionSpec as P

N = 6144


def mirror_pairs(n_recv, n_shot, flip):
    pairs = []
    for i in range(n_recv):
        for j in range(n_shot):
            h = (i % 2) ^ flip
            pairs.append((j * n_recv + i, (i // 2) * n_recv + 2 * j + h))
    return pairs


def gather_line(block):
    n_line = lax.axis_size("zl")
    line_index = lax.axis_index("zl")
    from_left, from_right = [], []
    rightward, leftward = block, block
    for _ in range(n_line - 1):
        rightward = lax.ppermute(rightward, "zl", [(k, k + 1) for k in range(n_line - 1)])
        leftward = lax.ppermute(leftward, "zl", [(k + 1, k) for k in range(n_line - 1)])
        from_left.append(rightward)
        from_right.append(leftward)
    sequence = jnp.stack(from_left[::-1] + [block] + from_right)
    mine = lax.dynamic_slice_in_dim(sequence, n_line - 1 - line_index, n_line, 0)
    other = lax.ppermute(mine, "core", [(0, 1), (1, 0)])
    return mine, other


def local(pressure):
    n_shot = lax.axis_size("zl") * lax.axis_size("core")
    n_half = lax.axis_size("y") * lax.axis_size("x")
    n_recv = 2 * n_half
    block_rows = pressure.shape[1]
    shot_index = lax.axis_index("zl") * lax.axis_size("core") + lax.axis_index("core")
    half_index = lax.axis_index("zh")
    recv_index = half_index * n_half + lax.axis_index("y") * lax.axis_size("x") + lax.axis_index("x")
    parity = recv_index % 2
    axes = ("zl", "core", "zh", "y", "x")

    arrived = []
    for flip in range(2):
        sent_half = (parity + flip) % 2
        piece = lax.dynamic_slice_in_dim(pressure, sent_half * block_rows, block_rows, 2)
        arrived.append(lax.ppermute(piece, axes, mirror_pairs(n_recv, n_shot, flip)))
    upper = jnp.where(parity == 0, arrived[0], arrived[1])
    lower = jnp.where(parity == 0, arrived[1], arrived[0])
    mirror = jnp.concatenate([upper, lower], axis=1)
    symmetric = (
        (pressure.astype(jnp.float32) + jnp.swapaxes(mirror, 1, 2).astype(jnp.float32)) * 0.5
    ).astype(jnp.bfloat16)

    partner_block = lax.ppermute(symmetric, "zh", [(0, 1), (1, 0)])
    top = jnp.where(half_index == 0, symmetric, partner_block)
    bottom = jnp.where(half_index == 0, partner_block, symmetric)
    pieces = jnp.swapaxes(jnp.stack([top, bottom]), 1, 2)
    panels = lax.all_gather(pieces, ("y", "x"), axis=1, tiled=False)
    mine, other = gather_line(symmetric)
    core_index = lax.axis_index("core")
    n_line = mine.shape[0]
    parts, rows, cols = symmetric.shape
    natural = jnp.where(
        core_index == 0, jnp.stack([mine, other], axis=1), jnp.stack([other, mine], axis=1)
    ).reshape((2 * n_line,) + symmetric.shape)

    panel = panels.reshape(2 * n_line, 2 * rows, parts, cols)
    terms = jnp.einsum("jpxc,jcqn->pqxn", natural, panel, preferred_element_type=jnp.float32)
    factor = 1.0 / math.sqrt(N)
    real = (terms[0, 0] - terms[1, 1]) * factor
    imag = (terms[0, 1] + terms[1, 0]) * factor
    return jnp.stack([real, imag])


def solution(mesh):
    n_shot, n_recv = mesh.devices.shape
    n_x = 4
    split = Mesh(
        mesh.devices.reshape(n_shot // 2, 2, 2, n_recv // (2 * n_x), n_x),
        ("zl", "core", "zh", "y", "x"),
    )
    placed = P(None, ("zh", "y", "x"), ("zl", "core"))
    return jax.shard_map(local, mesh=split, in_specs=(placed,), out_specs=placed, check_vma=False)
```

```python
import math

import jax
import jax.numpy as jnp
from jax import lax
from jax.sharding import Mesh
from jax.sharding import PartitionSpec as P

N = 6144


def mirror_pairs(n_recv, n_shot, flip):
    pairs = []
    for i in range(n_recv):
        for j in range(n_shot):
            h = (i % 2) ^ flip
            pairs.append((j * n_recv + i, (i // 2) * n_recv + 2 * j + h))
    return pairs


def gather_line(block):
    n_line = lax.axis_size("zl")
    line_index = lax.axis_index("zl")
    from_left, from_right = [], []
    rightward, leftward = block, block
    for _ in range(n_line - 1):
        rightward = lax.ppermute(rightward, "zl", [(k, k + 1) for k in range(n_line - 1)])
        leftward = lax.ppermute(leftward, "zl", [(k + 1, k) for k in range(n_line - 1)])
        from_left.append(rightward)
        from_right.append(leftward)
    sequence = jnp.stack(from_left[::-1] + [block] + from_right)
    mine = lax.dynamic_slice_in_dim(sequence, n_line - 1 - line_index, n_line, 0)
    other = lax.ppermute(mine, "core", [(0, 1), (1, 0)])
    return mine, other


def local(pressure):
    n_shot = lax.axis_size("zl") * lax.axis_size("core")
    n_half = lax.axis_size("y") * lax.axis_size("x")
    n_recv = 2 * n_half
    block_rows = pressure.shape[1]
    shot_index = lax.axis_index("zl") * lax.axis_size("core") + lax.axis_index("core")
    half_index = lax.axis_index("zh")
    recv_index = half_index * n_half + lax.axis_index("y") * lax.axis_size("x") + lax.axis_index("x")
    parity = recv_index % 2
    axes = ("zl", "core", "zh", "y", "x")

    arrived = []
    for flip in range(2):
        sent_half = (parity + flip) % 2
        piece = lax.dynamic_slice_in_dim(pressure, sent_half * block_rows, block_rows, 2)
        arrived.append(lax.ppermute(piece, axes, mirror_pairs(n_recv, n_shot, flip)))
    upper = jnp.where(parity == 0, arrived[0], arrived[1])
    lower = jnp.where(parity == 0, arrived[1], arrived[0])
    mirror = jnp.concatenate([upper, lower], axis=1)
    symmetric = (
        (pressure.astype(jnp.float32) + jnp.swapaxes(mirror, 1, 2).astype(jnp.float32)) * 0.5
    ).astype(jnp.bfloat16)

    partner_block = lax.ppermute(symmetric, "zh", [(0, 1), (1, 0)])
    top = jnp.where(half_index == 0, symmetric, partner_block)
    bottom = jnp.where(half_index == 0, partner_block, symmetric)
    pieces = jnp.swapaxes(jnp.stack([top, bottom]), 1, 2)
    n_plane = lax.axis_size("y") * lax.axis_size("x")
    plane_index = lax.axis_index("y") * lax.axis_size("x") + lax.axis_index("x")
    slots = jnp.zeros((pieces.shape[0], n_plane) + pieces.shape[1:], pieces.dtype)
    slots = lax.dynamic_update_slice_in_dim(slots, pieces[:, None], plane_index, 1)
    panels = lax.psum(slots, ("y", "x"))
    mine, other = gather_line(symmetric)
    core_index = lax.axis_index("core")
    n_line = mine.shape[0]
    parts, rows, cols = symmetric.shape
    natural = jnp.where(
        core_index == 0, jnp.stack([mine, other], axis=1), jnp.stack([other, mine], axis=1)
    ).reshape((2 * n_line,) + symmetric.shape)

    def product(left, panel):
        panel = panel.reshape(n_line, 2 * rows, parts, cols)
        return jnp.einsum("jpxc,jcqn->pqxn", left, panel, preferred_element_type=jnp.float32)

    terms = product(natural[:n_line], panels[0]) + product(natural[n_line:], panels[1])
    factor = 1.0 / math.sqrt(N)
    real = (terms[0, 0] - terms[1, 1]) * factor
    imag = (terms[0, 1] + terms[1, 0]) * factor
    return jnp.stack([real, imag])


def solution(mesh):
    n_shot, n_recv = mesh.devices.shape
    n_x = 4
    split = Mesh(
        mesh.devices.reshape(n_shot // 2, 2, 2, n_recv // (2 * n_x), n_x),
        ("zl", "core", "zh", "y", "x"),
    )
    placed = P(None, ("zh", "y", "x"), ("zl", "core"))
    return jax.shard_map(local, mesh=split, in_specs=(placed,), out_specs=placed, check_vma=False)
```

```python
import math

import jax
import jax.numpy as jnp
from jax import lax
from jax.sharding import Mesh
from jax.sharding import PartitionSpec as P

N = 6144


def mirror_pairs(n_recv, n_shot, flip):
    pairs = []
    for i in range(n_recv):
        for j in range(n_shot):
            h = (i % 2) ^ flip
            pairs.append((j * n_recv + i, (i // 2) * n_recv + 2 * j + h))
    return pairs


def gather_line(block):
    n_line = lax.axis_size("zl")
    line_index = lax.axis_index("zl")
    from_left, from_right = [], []
    rightward, leftward = block, block
    for _ in range(n_line - 1):
        rightward = lax.ppermute(rightward, "zl", [(k, k + 1) for k in range(n_line - 1)])
        leftward = lax.ppermute(leftward, "zl", [(k + 1, k) for k in range(n_line - 1)])
        from_left.append(rightward)
        from_right.append(leftward)
    sequence = jnp.stack(from_left[::-1] + [block] + from_right)
    mine = lax.dynamic_slice_in_dim(sequence, n_line - 1 - line_index, n_line, 0)
    other = lax.ppermute(mine, "core", [(0, 1), (1, 0)])
    return mine, other


def local(pressure):
    n_shot = lax.axis_size("zl") * lax.axis_size("core")
    n_half = lax.axis_size("y") * lax.axis_size("x")
    n_recv = 2 * n_half
    block_rows = pressure.shape[1]
    shot_index = lax.axis_index("zl") * lax.axis_size("core") + lax.axis_index("core")
    half_index = lax.axis_index("zh")
    recv_index = half_index * n_half + lax.axis_index("y") * lax.axis_size("x") + lax.axis_index("x")
    parity = recv_index % 2
    axes = ("zl", "core", "zh", "y", "x")

    arrived = []
    for flip in range(2):
        sent_half = (parity + flip) % 2
        piece = lax.dynamic_slice_in_dim(pressure, sent_half * block_rows, block_rows, 2)
        arrived.append(lax.ppermute(piece, axes, mirror_pairs(n_recv, n_shot, flip)))
    upper = jnp.where(parity == 0, arrived[0], arrived[1])
    lower = jnp.where(parity == 0, arrived[1], arrived[0])
    mirror = jnp.concatenate([upper, lower], axis=1)
    symmetric = (
        (pressure.astype(jnp.float32) + jnp.swapaxes(mirror, 1, 2).astype(jnp.float32)) * 0.5
    ).astype(jnp.bfloat16)

    stacked = lax.all_to_all(jnp.stack([symmetric, symmetric]), "zh", 0, 0, tiled=True)
    pieces = jnp.swapaxes(stacked, 1, 2)
    panels = lax.all_gather(pieces, ("y", "x"), axis=1, tiled=False)
    mine, other = gather_line(symmetric)
    core_index = lax.axis_index("core")
    n_line = mine.shape[0]
    parts, rows, cols = symmetric.shape
    natural = jnp.where(
        core_index == 0, jnp.stack([mine, other], axis=1), jnp.stack([other, mine], axis=1)
    ).reshape((2 * n_line,) + symmetric.shape)

    def product(left, panel):
        panel = panel.reshape(n_line, 2 * rows, parts, cols)
        return jnp.einsum("jpxc,jcqn->pqxn", left, panel, preferred_element_type=jnp.float32)

    terms = product(natural[:n_line], panels[0]) + product(natural[n_line:], panels[1])
    factor = 1.0 / math.sqrt(N)
    real = (terms[0, 0] - terms[1, 1]) * factor
    imag = (terms[0, 1] + terms[1, 0]) * factor
    return jnp.stack([real, imag])


def solution(mesh):
    n_shot, n_recv = mesh.devices.shape
    n_x = 4
    split = Mesh(
        mesh.devices.reshape(n_shot // 2, 2, 2, n_recv // (2 * n_x), n_x),
        ("zl", "core", "zh", "y", "x"),
    )
    placed = P(None, ("zh", "y", "x"), ("zl", "core"))
    return jax.shard_map(local, mesh=split, in_specs=(placed,), out_specs=placed, check_vma=False)
```

```python
import functools
import math

import jax
import jax.numpy as jnp
from jax import lax
from jax.sharding import Mesh
from jax.sharding import PartitionSpec as P
from jax.experimental import pallas as pl
from jax.experimental.pallas import tpu as pltpu

N = 6144


def mirror_pairs(n_recv, n_shot, flip):
    pairs = []
    for i in range(n_recv):
        for j in range(n_shot):
            h = (i % 2) ^ flip
            pairs.append((j * n_recv + i, (i // 2) * n_recv + 2 * j + h))
    return pairs


def gather_line(block):
    n_line = lax.axis_size("zl")
    line_index = lax.axis_index("zl")
    from_left, from_right = [], []
    rightward, leftward = block, block
    for _ in range(n_line - 1):
        rightward = lax.ppermute(rightward, "zl", [(k, k + 1) for k in range(n_line - 1)])
        leftward = lax.ppermute(leftward, "zl", [(k + 1, k) for k in range(n_line - 1)])
        from_left.append(rightward)
        from_right.append(leftward)
    sequence = jnp.stack(from_left[::-1] + [block] + from_right)
    mine = lax.dynamic_slice_in_dim(sequence, n_line - 1 - line_index, n_line, 0)
    other = lax.ppermute(mine, "core", [(0, 1), (1, 0)])
    return mine, other


def product_kernel(left_ref, panel_ref, out_ref, *, n_block, width, factor):
    acc = [[None, None], [None, None]]
    for half in range(2):
        for block in range(n_block):
            for p in range(2):
                lhs = left_ref[half * n_block + block, p, :, :]
                for q in range(2):
                    rhs = panel_ref[half, q, pl.ds(block * width, width), :]
                    term = jnp.dot(lhs, rhs, preferred_element_type=jnp.float32)
                    acc[p][q] = term if acc[p][q] is None else acc[p][q] + term
    out_ref[0, :, :] = (acc[0][0] - acc[1][1]) * factor
    out_ref[1, :, :] = (acc[0][1] + acc[1][0]) * factor


def product(left, panels, factor):
    n_blocks, parts, rows, width = left.shape
    cols = panels.shape[-1]
    kernel = functools.partial(product_kernel, n_block=n_blocks // 2, width=width, factor=factor)
    return pl.pallas_call(
        kernel,
        out_shape=jax.ShapeDtypeStruct((2, rows, cols), jnp.float32),
        in_specs=[pl.BlockSpec(memory_space=pltpu.VMEM)] * 2,
        out_specs=pl.BlockSpec(memory_space=pltpu.VMEM),
        cost_estimate=pl.CostEstimate(
            flops=2 * 4 * rows * cols * width * n_blocks,
            transcendentals=0,
            bytes_accessed=2 * (left.size + panels.size) + 4 * 2 * rows * cols,
        ),
    )(left, panels)


def local(pressure):
    n_shot = lax.axis_size("zl") * lax.axis_size("core")
    n_half = lax.axis_size("y") * lax.axis_size("x")
    n_recv = 2 * n_half
    block_rows = pressure.shape[1]
    shot_index = lax.axis_index("zl") * lax.axis_size("core") + lax.axis_index("core")
    half_index = lax.axis_index("zh")
    recv_index = half_index * n_half + lax.axis_index("y") * lax.axis_size("x") + lax.axis_index("x")
    parity = recv_index % 2
    axes = ("zl", "core", "zh", "y", "x")

    arrived = []
    for flip in range(2):
        sent_half = (parity + flip) % 2
        piece = lax.dynamic_slice_in_dim(pressure, sent_half * block_rows, block_rows, 2)
        arrived.append(lax.ppermute(piece, axes, mirror_pairs(n_recv, n_shot, flip)))
    upper = jnp.where(parity == 0, arrived[0], arrived[1])
    lower = jnp.where(parity == 0, arrived[1], arrived[0])
    mirror = jnp.concatenate([upper, lower], axis=1)
    symmetric = (
        (pressure.astype(jnp.float32) + jnp.swapaxes(mirror, 1, 2).astype(jnp.float32)) * 0.5
    ).astype(jnp.bfloat16)

    partner_block = lax.ppermute(symmetric, "zh", [(0, 1), (1, 0)])
    top = jnp.where(half_index == 0, symmetric, partner_block)
    bottom = jnp.where(half_index == 0, partner_block, symmetric)
    panels = lax.all_gather(jnp.stack([top, bottom]), ("y", "x"), axis=2, tiled=True)
    mine, other = gather_line(symmetric)
    core_index = lax.axis_index("core")
    n_line = mine.shape[0]
    natural = jnp.where(
        core_index == 0, jnp.stack([mine, other], axis=1), jnp.stack([other, mine], axis=1)
    ).reshape((2 * n_line,) + symmetric.shape)
    return product(natural, panels, 1.0 / math.sqrt(N))


def solution(mesh):
    n_shot, n_recv = mesh.devices.shape
    n_x = 4
    split = Mesh(
        mesh.devices.reshape(n_shot // 2, 2, 2, n_recv // (2 * n_x), n_x),
        ("zl", "core", "zh", "y", "x"),
    )
    placed = P(None, ("zh", "y", "x"), ("zl", "core"))
    return jax.shard_map(local, mesh=split, in_specs=(placed,), out_specs=placed, check_vma=False)
```

```python
import functools
import math

import jax
import jax.numpy as jnp
from jax import lax
from jax.sharding import Mesh
from jax.sharding import PartitionSpec as P
from jax.experimental import pallas as pl
from jax.experimental.pallas import tpu as pltpu

N = 6144


def mirror_pairs(n_recv, n_shot, flip):
    pairs = []
    for i in range(n_recv):
        for j in range(n_shot):
            h = (i % 2) ^ flip
            pairs.append((j * n_recv + i, (i // 2) * n_recv + 2 * j + h))
    return pairs


def gather_line(block):
    n_line = lax.axis_size("zl")
    line_index = lax.axis_index("zl")
    from_left, from_right = [], []
    rightward, leftward = block, block
    for _ in range(n_line - 1):
        rightward = lax.ppermute(rightward, "zl", [(k, k + 1) for k in range(n_line - 1)])
        leftward = lax.ppermute(leftward, "zl", [(k + 1, k) for k in range(n_line - 1)])
        from_left.append(rightward)
        from_right.append(leftward)
    sequence = jnp.stack(from_left[::-1] + [block] + from_right)
    mine = lax.dynamic_slice_in_dim(sequence, n_line - 1 - line_index, n_line, 0)
    other = lax.ppermute(mine, "core", [(0, 1), (1, 0)])
    return mine, other


def product_kernel(left_ref, panel_ref, out_ref, acc_ref, *, n_block, width, factor):
    for half in range(2):
        for block in range(n_block):
            rhs = panel_ref[half, pl.ds(block * width, width), :]
            for p in range(2):
                term = jnp.dot(left_ref[half * n_block + block, p, :, :], rhs, preferred_element_type=jnp.float32)
                if half == 0 and block == 0:
                    acc_ref[p] = term
                else:
                    acc_ref[p] += term
    cols = out_ref.shape[-1]
    out_ref[0, :, :] = (acc_ref[0, :, :cols] - acc_ref[1, :, cols:]) * factor
    out_ref[1, :, :] = (acc_ref[0, :, cols:] + acc_ref[1, :, :cols]) * factor


def product(left, panels, factor):
    n_blocks, parts, rows, width = left.shape
    cols = panels.shape[-1] // 2
    kernel = functools.partial(product_kernel, n_block=n_blocks // 2, width=width, factor=factor)
    return pl.pallas_call(
        kernel,
        out_shape=jax.ShapeDtypeStruct((2, rows, cols), jnp.float32),
        in_specs=[pl.BlockSpec(memory_space=pltpu.VMEM)] * 2,
        out_specs=pl.BlockSpec(memory_space=pltpu.VMEM),
        scratch_shapes=[pltpu.VMEM((2, rows, 2 * cols), jnp.float32)],
        cost_estimate=pl.CostEstimate(
            flops=2 * 4 * rows * cols * width * n_blocks,
            transcendentals=0,
            bytes_accessed=2 * (left.size + panels.size) + 4 * 2 * rows * cols,
        ),
    )(left, panels)


def local(pressure):
    n_shot = lax.axis_size("zl") * lax.axis_size("core")
    n_half = lax.axis_size("y") * lax.axis_size("x")
    n_recv = 2 * n_half
    block_rows = pressure.shape[1]
    shot_index = lax.axis_index("zl") * lax.axis_size("core") + lax.axis_index("core")
    half_index = lax.axis_index("zh")
    recv_index = half_index * n_half + lax.axis_index("y") * lax.axis_size("x") + lax.axis_index("x")
    parity = recv_index % 2
    axes = ("zl", "core", "zh", "y", "x")

    arrived = []
    for flip in range(2):
        sent_half = (parity + flip) % 2
        piece = lax.dynamic_slice_in_dim(pressure, sent_half * block_rows, block_rows, 2)
        arrived.append(lax.ppermute(piece, axes, mirror_pairs(n_recv, n_shot, flip)))
    upper = jnp.where(parity == 0, arrived[0], arrived[1])
    lower = jnp.where(parity == 0, arrived[1], arrived[0])
    mirror = jnp.concatenate([upper, lower], axis=1)
    symmetric = (
        (pressure.astype(jnp.float32) + jnp.swapaxes(mirror, 1, 2).astype(jnp.float32)) * 0.5
    ).astype(jnp.bfloat16)

    partner_block = lax.ppermute(symmetric, "zh", [(0, 1), (1, 0)])
    top = jnp.where(half_index == 0, symmetric, partner_block)
    bottom = jnp.where(half_index == 0, partner_block, symmetric)
    pieces = jnp.swapaxes(jnp.stack([top, bottom]), 1, 2)
    panels = lax.all_gather(pieces, ("y", "x"), axis=1, tiled=True)
    panels = panels.reshape(panels.shape[0], panels.shape[1], -1)
    mine, other = gather_line(symmetric)
    core_index = lax.axis_index("core")
    n_line = mine.shape[0]
    natural = jnp.where(
        core_index == 0, jnp.stack([mine, other], axis=1), jnp.stack([other, mine], axis=1)
    ).reshape((2 * n_line,) + symmetric.shape)
    return product(natural, panels, 1.0 / math.sqrt(N))


def solution(mesh):
    n_shot, n_recv = mesh.devices.shape
    n_x = 4
    split = Mesh(
        mesh.devices.reshape(n_shot // 2, 2, 2, n_recv // (2 * n_x), n_x),
        ("zl", "core", "zh", "y", "x"),
    )
    placed = P(None, ("zh", "y", "x"), ("zl", "core"))
    return jax.shard_map(local, mesh=split, in_specs=(placed,), out_specs=placed, check_vma=False)
```

```python
import functools
import math

import jax
import jax.numpy as jnp
from jax import lax
from jax.sharding import Mesh
from jax.sharding import PartitionSpec as P
from jax.experimental import pallas as pl
from jax.experimental.pallas import tpu as pltpu

N = 6144


def mirror_pairs(n_recv, n_shot, flip):
    pairs = []
    for i in range(n_recv):
        for j in range(n_shot):
            h = (i % 2) ^ flip
            pairs.append((j * n_recv + i, (i // 2) * n_recv + 2 * j + h))
    return pairs


def gather_line(block):
    n_line = lax.axis_size("zl")
    line_index = lax.axis_index("zl")
    from_left, from_right = [], []
    rightward, leftward = block, block
    for _ in range(n_line - 1):
        rightward = lax.ppermute(rightward, "zl", [(k, k + 1) for k in range(n_line - 1)])
        leftward = lax.ppermute(leftward, "zl", [(k + 1, k) for k in range(n_line - 1)])
        from_left.append(rightward)
        from_right.append(leftward)
    sequence = jnp.stack(from_left[::-1] + [block] + from_right)
    mine = lax.dynamic_slice_in_dim(sequence, n_line - 1 - line_index, n_line, 0)
    other = lax.ppermute(mine, "core", [(0, 1), (1, 0)])
    return mine, other


def product_kernel(left_ref, panel_ref, out_ref, acc_ref, *, n_block, width, factor):
    for half in range(2):
        for block in range(n_block):
            for p in range(2):
                lhs = left_ref[half * n_block + block, p, :, :]
                for q in range(2):
                    rhs = panel_ref[half, q, pl.ds(block * width, width), :]
                    term = jnp.dot(lhs, rhs, preferred_element_type=jnp.float32)
                    if half == 0 and block == 0:
                        acc_ref[p, q] = term
                    else:
                        acc_ref[p, q] += term
    out_ref[0, :, :] = (acc_ref[0, 0] - acc_ref[1, 1]) * factor
    out_ref[1, :, :] = (acc_ref[0, 1] + acc_ref[1, 0]) * factor


def product(left, panels, factor):
    n_blocks, parts, rows, width = left.shape
    cols = panels.shape[-1]
    kernel = functools.partial(product_kernel, n_block=n_blocks // 2, width=width, factor=factor)
    return pl.pallas_call(
        kernel,
        out_shape=jax.ShapeDtypeStruct((2, rows, cols), jnp.float32),
        in_specs=[pl.BlockSpec(memory_space=pltpu.VMEM)] * 2,
        out_specs=pl.BlockSpec(memory_space=pltpu.VMEM),
        scratch_shapes=[pltpu.VMEM((2, 2, rows, cols), jnp.float32)],
        cost_estimate=pl.CostEstimate(
            flops=2 * 4 * rows * cols * width * n_blocks,
            transcendentals=0,
            bytes_accessed=2 * (left.size + panels.size) + 4 * 2 * rows * cols,
        ),
    )(left, panels)


def local(pressure):
    n_shot = lax.axis_size("zl") * lax.axis_size("core")
    n_half = lax.axis_size("y") * lax.axis_size("x")
    n_recv = 2 * n_half
    block_rows = pressure.shape[1]
    shot_index = lax.axis_index("zl") * lax.axis_size("core") + lax.axis_index("core")
    half_index = lax.axis_index("zh")
    recv_index = half_index * n_half + lax.axis_index("y") * lax.axis_size("x") + lax.axis_index("x")
    parity = recv_index % 2
    axes = ("zl", "core", "zh", "y", "x")

    arrived = []
    for flip in range(2):
        sent_half = (parity + flip) % 2
        piece = lax.dynamic_slice_in_dim(pressure, sent_half * block_rows, block_rows, 2)
        arrived.append(lax.ppermute(piece, axes, mirror_pairs(n_recv, n_shot, flip)))
    upper = jnp.where(parity == 0, arrived[0], arrived[1])
    lower = jnp.where(parity == 0, arrived[1], arrived[0])
    mirror = jnp.concatenate([upper, lower], axis=1)
    symmetric = (
        (pressure.astype(jnp.float32) + jnp.swapaxes(mirror, 1, 2).astype(jnp.float32)) * 0.5
    ).astype(jnp.bfloat16)

    partner_block = lax.ppermute(symmetric, "zh", [(0, 1), (1, 0)])
    top = jnp.where(half_index == 0, symmetric, partner_block)
    bottom = jnp.where(half_index == 0, partner_block, symmetric)
    panels = lax.all_gather(jnp.stack([top, bottom]), ("y", "x"), axis=2, tiled=True)
    mine, other = gather_line(symmetric)
    core_index = lax.axis_index("core")
    n_line = mine.shape[0]
    natural = jnp.where(
        core_index == 0, jnp.stack([mine, other], axis=1), jnp.stack([other, mine], axis=1)
    ).reshape((2 * n_line,) + symmetric.shape)
    return product(natural, panels, 1.0 / math.sqrt(N))


def solution(mesh):
    n_shot, n_recv = mesh.devices.shape
    n_x = 4
    split = Mesh(
        mesh.devices.reshape(n_shot // 2, 2, 2, n_recv // (2 * n_x), n_x),
        ("zl", "core", "zh", "y", "x"),
    )
    placed = P(None, ("zh", "y", "x"), ("zl", "core"))
    return jax.shard_map(local, mesh=split, in_specs=(placed,), out_specs=placed, check_vma=False)
```

```python
import functools
import math

import jax
import jax.numpy as jnp
from jax import lax
from jax.sharding import Mesh
from jax.sharding import PartitionSpec as P
from jax.experimental import pallas as pl
from jax.experimental.pallas import tpu as pltpu

N = 6144


def mirror_pairs(n_recv, n_shot, flip):
    pairs = []
    for i in range(n_recv):
        for j in range(n_shot):
            h = (i % 2) ^ flip
            pairs.append((j * n_recv + i, (i // 2) * n_recv + 2 * j + h))
    return pairs


def gather_line(block):
    n_line = lax.axis_size("zl")
    line_index = lax.axis_index("zl")
    from_left, from_right = [], []
    rightward, leftward = block, block
    for _ in range(n_line - 1):
        rightward = lax.ppermute(rightward, "zl", [(k, k + 1) for k in range(n_line - 1)])
        leftward = lax.ppermute(leftward, "zl", [(k + 1, k) for k in range(n_line - 1)])
        from_left.append(rightward)
        from_right.append(leftward)
    sequence = jnp.stack(from_left[::-1] + [block] + from_right)
    mine = lax.dynamic_slice_in_dim(sequence, n_line - 1 - line_index, n_line, 0)
    other = lax.ppermute(mine, "core", [(0, 1), (1, 0)])
    return mine, other


def product_kernel(left_ref, panel_hbm, out_ref, buffers, copied, acc_ref, *, n_block, width, factor):
    chunk_rows = n_block * width
    n_chunks = panel_hbm.shape[2] // chunk_rows
    chunks = [(half, k) for half in range(2) for k in range(n_chunks)]

    def fetch(index):
        half, k = chunks[index]
        return pltpu.make_async_copy(
            panel_hbm.at[half, :, pl.ds(k * chunk_rows, chunk_rows), :],
            buffers.at[index % 2],
            copied.at[index % 2],
        )

    fetch(0).start()
    for index, (half, k) in enumerate(chunks):
        if index + 1 < len(chunks):
            fetch(index + 1).start()
        fetch(index).wait()
        for block in range(n_block):
            lhs_index = (half * n_chunks + k) * n_block + block
            for p in range(2):
                lhs = left_ref[lhs_index, p, :, :]
                for q in range(2):
                    rhs = buffers[index % 2, q, pl.ds(block * width, width), :]
                    term = jnp.dot(lhs, rhs, preferred_element_type=jnp.float32)
                    if index == 0 and block == 0:
                        acc_ref[p, q] = term
                    else:
                        acc_ref[p, q] += term
    out_ref[0, :, :] = (acc_ref[0, 0] - acc_ref[1, 1]) * factor
    out_ref[1, :, :] = (acc_ref[0, 1] + acc_ref[1, 0]) * factor


def product(left, panels, factor):
    n_blocks, parts, rows, width = left.shape
    cols = panels.shape[-1]
    n_block = n_blocks // 4
    kernel = functools.partial(product_kernel, n_block=n_block, width=width, factor=factor)
    return pl.pallas_call(
        kernel,
        out_shape=jax.ShapeDtypeStruct((2, rows, cols), jnp.float32),
        in_specs=[pl.BlockSpec(memory_space=pltpu.VMEM), pl.BlockSpec(memory_space=pl.ANY)],
        out_specs=pl.BlockSpec(memory_space=pltpu.VMEM),
        scratch_shapes=[
            pltpu.VMEM((2, parts, n_block * width, cols), panels.dtype),
            pltpu.SemaphoreType.DMA((2,)),
            pltpu.VMEM((2, 2, rows, cols), jnp.float32),
        ],
        cost_estimate=pl.CostEstimate(
            flops=2 * 4 * rows * cols * width * n_blocks,
            transcendentals=0,
            bytes_accessed=2 * (left.size + panels.size) + 4 * 2 * rows * cols,
        ),
    )(left, panels)


def local(pressure):
    n_shot = lax.axis_size("zl") * lax.axis_size("core")
    n_half = lax.axis_size("y") * lax.axis_size("x")
    n_recv = 2 * n_half
    block_rows = pressure.shape[1]
    shot_index = lax.axis_index("zl") * lax.axis_size("core") + lax.axis_index("core")
    half_index = lax.axis_index("zh")
    recv_index = half_index * n_half + lax.axis_index("y") * lax.axis_size("x") + lax.axis_index("x")
    parity = recv_index % 2
    axes = ("zl", "core", "zh", "y", "x")

    arrived = []
    for flip in range(2):
        sent_half = (parity + flip) % 2
        piece = lax.dynamic_slice_in_dim(pressure, sent_half * block_rows, block_rows, 2)
        arrived.append(lax.ppermute(piece, axes, mirror_pairs(n_recv, n_shot, flip)))
    upper = jnp.where(parity == 0, arrived[0], arrived[1])
    lower = jnp.where(parity == 0, arrived[1], arrived[0])
    mirror = jnp.concatenate([upper, lower], axis=1)
    symmetric = (
        (pressure.astype(jnp.float32) + jnp.swapaxes(mirror, 1, 2).astype(jnp.float32)) * 0.5
    ).astype(jnp.bfloat16)

    partner_block = lax.ppermute(symmetric, "zh", [(0, 1), (1, 0)])
    top = jnp.where(half_index == 0, symmetric, partner_block)
    bottom = jnp.where(half_index == 0, partner_block, symmetric)
    panels = lax.all_gather(jnp.stack([top, bottom]), ("y", "x"), axis=2, tiled=True)
    mine, other = gather_line(symmetric)
    core_index = lax.axis_index("core")
    n_line = mine.shape[0]
    natural = jnp.where(
        core_index == 0, jnp.stack([mine, other], axis=1), jnp.stack([other, mine], axis=1)
    ).reshape((2 * n_line,) + symmetric.shape)
    return product(natural, panels, 1.0 / math.sqrt(N))


def solution(mesh):
    n_shot, n_recv = mesh.devices.shape
    n_x = 4
    split = Mesh(
        mesh.devices.reshape(n_shot // 2, 2, 2, n_recv // (2 * n_x), n_x),
        ("zl", "core", "zh", "y", "x"),
    )
    placed = P(None, ("zh", "y", "x"), ("zl", "core"))
    return jax.shard_map(local, mesh=split, in_specs=(placed,), out_specs=placed, check_vma=False)
```

```python
import functools
import math

import jax
import jax.numpy as jnp
from jax import lax
from jax.sharding import Mesh
from jax.sharding import PartitionSpec as P
from jax.experimental import pallas as pl
from jax.experimental.pallas import tpu as pltpu

N = 6144


def mirror_pairs(n_recv, n_shot, flip):
    pairs = []
    for i in range(n_recv):
        for j in range(n_shot):
            h = (i % 2) ^ flip
            pairs.append((j * n_recv + i, (i // 2) * n_recv + 2 * j + h))
    return pairs


def gather_line(block):
    n_line = lax.axis_size("zl")
    line_index = lax.axis_index("zl")
    from_left, from_right = [], []
    rightward, leftward = block, block
    for _ in range(n_line - 1):
        rightward = lax.ppermute(rightward, "zl", [(k, k + 1) for k in range(n_line - 1)])
        leftward = lax.ppermute(leftward, "zl", [(k + 1, k) for k in range(n_line - 1)])
        from_left.append(rightward)
        from_right.append(leftward)
    sequence = jnp.stack(from_left[::-1] + [block] + from_right)
    mine = lax.dynamic_slice_in_dim(sequence, n_line - 1 - line_index, n_line, 0)
    other = lax.ppermute(mine, "core", [(0, 1), (1, 0)])
    return mine, other


def product_kernel(left_ref, panel_hbm, out_ref, buffers, copied, acc_ref, *, n_block, width, factor):
    chunk_rows = n_block * width
    n_chunks = panel_hbm.shape[2] // chunk_rows
    chunks = [(half, k) for half in range(2) for k in range(n_chunks)]

    def fetch(index):
        half, k = chunks[index]
        return pltpu.make_async_copy(
            panel_hbm.at[half, :, pl.ds(k * chunk_rows, chunk_rows), :],
            buffers.at[index % 2],
            copied.at[index % 2],
        )

    fetch(0).start()
    for index, (half, k) in enumerate(chunks):
        if index + 1 < len(chunks):
            fetch(index + 1).start()
        fetch(index).wait()
        for block in range(n_block):
            lhs_index = (half * n_chunks + k) * n_block + block
            lhs = left_ref[lhs_index].reshape(-1, left_ref.shape[-1])
            for q in range(2):
                rhs = buffers[index % 2, q, pl.ds(block * width, width), :]
                term = jnp.dot(lhs, rhs, preferred_element_type=jnp.float32)
                if index == 0 and block == 0:
                    acc_ref[q] = term
                else:
                    acc_ref[q] += term
    rows = out_ref.shape[1]
    out_ref[0, :, :] = (acc_ref[0, :rows] - acc_ref[1, rows:]) * factor
    out_ref[1, :, :] = (acc_ref[1, :rows] + acc_ref[0, rows:]) * factor


def product(left, panels, factor):
    n_blocks, parts, rows, width = left.shape
    cols = panels.shape[-1]
    n_block = n_blocks // 4
    kernel = functools.partial(product_kernel, n_block=n_block, width=width, factor=factor)
    return pl.pallas_call(
        kernel,
        out_shape=jax.ShapeDtypeStruct((2, rows, cols), jnp.float32),
        in_specs=[pl.BlockSpec(memory_space=pltpu.VMEM), pl.BlockSpec(memory_space=pl.ANY)],
        out_specs=pl.BlockSpec(memory_space=pltpu.VMEM),
        scratch_shapes=[
            pltpu.VMEM((2, parts, n_block * width, cols), panels.dtype),
            pltpu.SemaphoreType.DMA((2,)),
            pltpu.VMEM((2, parts * rows, cols), jnp.float32),
        ],
        cost_estimate=pl.CostEstimate(
            flops=2 * 4 * rows * cols * width * n_blocks,
            transcendentals=0,
            bytes_accessed=2 * (left.size + panels.size) + 4 * 2 * rows * cols,
        ),
    )(left, panels)


def local(pressure):
    n_shot = lax.axis_size("zl") * lax.axis_size("core")
    n_half = lax.axis_size("y") * lax.axis_size("x")
    n_recv = 2 * n_half
    block_rows = pressure.shape[1]
    shot_index = lax.axis_index("zl") * lax.axis_size("core") + lax.axis_index("core")
    half_index = lax.axis_index("zh")
    recv_index = half_index * n_half + lax.axis_index("y") * lax.axis_size("x") + lax.axis_index("x")
    parity = recv_index % 2
    axes = ("zl", "core", "zh", "y", "x")

    arrived = []
    for flip in range(2):
        sent_half = (parity + flip) % 2
        piece = lax.dynamic_slice_in_dim(pressure, sent_half * block_rows, block_rows, 2)
        arrived.append(lax.ppermute(piece, axes, mirror_pairs(n_recv, n_shot, flip)))
    upper = jnp.where(parity == 0, arrived[0], arrived[1])
    lower = jnp.where(parity == 0, arrived[1], arrived[0])
    mirror = jnp.concatenate([upper, lower], axis=1)
    symmetric = (
        (pressure.astype(jnp.float32) + jnp.swapaxes(mirror, 1, 2).astype(jnp.float32)) * 0.5
    ).astype(jnp.bfloat16)

    partner_block = lax.ppermute(symmetric, "zh", [(0, 1), (1, 0)])
    top = jnp.where(half_index == 0, symmetric, partner_block)
    bottom = jnp.where(half_index == 0, partner_block, symmetric)
    panels = lax.all_gather(jnp.stack([top, bottom]), ("y", "x"), axis=2, tiled=True)
    mine, other = gather_line(symmetric)
    core_index = lax.axis_index("core")
    n_line = mine.shape[0]
    natural = jnp.where(
        core_index == 0, jnp.stack([mine, other], axis=1), jnp.stack([other, mine], axis=1)
    ).reshape((2 * n_line,) + symmetric.shape)
    return product(natural, panels, 1.0 / math.sqrt(N))


def solution(mesh):
    n_shot, n_recv = mesh.devices.shape
    n_x = 4
    split = Mesh(
        mesh.devices.reshape(n_shot // 2, 2, 2, n_recv // (2 * n_x), n_x),
        ("zl", "core", "zh", "y", "x"),
    )
    placed = P(None, ("zh", "y", "x"), ("zl", "core"))
    return jax.shard_map(local, mesh=split, in_specs=(placed,), out_specs=placed, check_vma=False)
```

```python
import functools
import math

import jax
import jax.numpy as jnp
from jax import lax
from jax.sharding import Mesh
from jax.sharding import PartitionSpec as P
from jax.experimental import pallas as pl
from jax.experimental.pallas import tpu as pltpu

N = 6144


def mirror_pairs(n_recv, n_shot, flip):
    pairs = []
    for i in range(n_recv):
        for j in range(n_shot):
            h = (i % 2) ^ flip
            pairs.append((j * n_recv + i, (i // 2) * n_recv + 2 * j + h))
    return pairs


def gather_line(block):
    n_line = lax.axis_size("zl")
    line_index = lax.axis_index("zl")
    from_left, from_right = [], []
    rightward, leftward = block, block
    for _ in range(n_line - 1):
        rightward = lax.ppermute(rightward, "zl", [(k, k + 1) for k in range(n_line - 1)])
        leftward = lax.ppermute(leftward, "zl", [(k + 1, k) for k in range(n_line - 1)])
        from_left.append(rightward)
        from_right.append(leftward)
    sequence = jnp.stack(from_left[::-1] + [block] + from_right)
    mine = lax.dynamic_slice_in_dim(sequence, n_line - 1 - line_index, n_line, 0)
    other = lax.ppermute(mine, "core", [(0, 1), (1, 0)])
    return mine, other


def product_kernel(left_hbm, panel_hbm, out_ref, lefts, buffers, copied, acc_ref, *, n_block, width, factor):
    chunk_rows = n_block * width
    n_chunks = panel_hbm.shape[2] // chunk_rows
    chunks = [(half, k) for half in range(2) for k in range(n_chunks)]

    def fetch(index):
        half, k = chunks[index]
        return (
            pltpu.make_async_copy(
                panel_hbm.at[half, :, pl.ds(k * chunk_rows, chunk_rows), :],
                buffers.at[index % 2],
                copied.at[0, index % 2],
            ),
            pltpu.make_async_copy(
                left_hbm.at[pl.ds(index * n_block, n_block)], lefts.at[index % 2], copied.at[1, index % 2]
            ),
        )

    for copy in fetch(0):
        copy.start()
    for index, (half, k) in enumerate(chunks):
        if index + 1 < len(chunks):
            for copy in fetch(index + 1):
                copy.start()
        for copy in fetch(index):
            copy.wait()
        for block in range(n_block):
            for p in range(2):
                lhs = lefts[index % 2, block, p, :, :]
                for q in range(2):
                    rhs = buffers[index % 2, q, pl.ds(block * width, width), :]
                    term = jnp.dot(lhs, rhs, preferred_element_type=jnp.float32)
                    if index == 0 and block == 0:
                        acc_ref[p, q] = term
                    else:
                        acc_ref[p, q] += term
    out_ref[0, :, :] = (acc_ref[0, 0] - acc_ref[1, 1]) * factor
    out_ref[1, :, :] = (acc_ref[0, 1] + acc_ref[1, 0]) * factor


def product(left, panels, factor):
    n_blocks, parts, rows, width = left.shape
    cols = panels.shape[-1]
    n_block = n_blocks // 4
    kernel = functools.partial(product_kernel, n_block=n_block, width=width, factor=factor)
    return pl.pallas_call(
        kernel,
        out_shape=jax.ShapeDtypeStruct((2, rows, cols), jnp.float32),
        in_specs=[pl.BlockSpec(memory_space=pl.ANY), pl.BlockSpec(memory_space=pl.ANY)],
        out_specs=pl.BlockSpec(memory_space=pltpu.VMEM),
        scratch_shapes=[
            pltpu.VMEM((2, n_block, parts, rows, width), left.dtype),
            pltpu.VMEM((2, parts, n_block * width, cols), panels.dtype),
            pltpu.SemaphoreType.DMA((2, 2)),
            pltpu.VMEM((2, 2, rows, cols), jnp.float32),
        ],
        cost_estimate=pl.CostEstimate(
            flops=2 * 4 * rows * cols * width * n_blocks,
            transcendentals=0,
            bytes_accessed=2 * (left.size + panels.size) + 4 * 2 * rows * cols,
        ),
    )(left, panels)


def local(pressure):
    n_shot = lax.axis_size("zl") * lax.axis_size("core")
    n_half = lax.axis_size("y") * lax.axis_size("x")
    n_recv = 2 * n_half
    block_rows = pressure.shape[1]
    shot_index = lax.axis_index("zl") * lax.axis_size("core") + lax.axis_index("core")
    half_index = lax.axis_index("zh")
    recv_index = half_index * n_half + lax.axis_index("y") * lax.axis_size("x") + lax.axis_index("x")
    parity = recv_index % 2
    axes = ("zl", "core", "zh", "y", "x")

    arrived = []
    for flip in range(2):
        sent_half = (parity + flip) % 2
        piece = lax.dynamic_slice_in_dim(pressure, sent_half * block_rows, block_rows, 2)
        arrived.append(lax.ppermute(piece, axes, mirror_pairs(n_recv, n_shot, flip)))
    upper = jnp.where(parity == 0, arrived[0], arrived[1])
    lower = jnp.where(parity == 0, arrived[1], arrived[0])
    mirror = jnp.concatenate([upper, lower], axis=1)
    symmetric = (
        (pressure.astype(jnp.float32) + jnp.swapaxes(mirror, 1, 2).astype(jnp.float32)) * 0.5
    ).astype(jnp.bfloat16)

    partner_block = lax.ppermute(symmetric, "zh", [(0, 1), (1, 0)])
    top = jnp.where(half_index == 0, symmetric, partner_block)
    bottom = jnp.where(half_index == 0, partner_block, symmetric)
    panels = lax.all_gather(jnp.stack([top, bottom]), ("y", "x"), axis=2, tiled=True)
    mine, other = gather_line(symmetric)
    core_index = lax.axis_index("core")
    n_line = mine.shape[0]
    natural = jnp.where(
        core_index == 0, jnp.stack([mine, other], axis=1), jnp.stack([other, mine], axis=1)
    ).reshape((2 * n_line,) + symmetric.shape)
    return product(natural, panels, 1.0 / math.sqrt(N))


def solution(mesh):
    n_shot, n_recv = mesh.devices.shape
    n_x = 4
    split = Mesh(
        mesh.devices.reshape(n_shot // 2, 2, 2, n_recv // (2 * n_x), n_x),
        ("zl", "core", "zh", "y", "x"),
    )
    placed = P(None, ("zh", "y", "x"), ("zl", "core"))
    return jax.shard_map(local, mesh=split, in_specs=(placed,), out_specs=placed, check_vma=False)
```

```python
import functools
import math

import jax
import jax.numpy as jnp
from jax import lax
from jax.sharding import Mesh
from jax.sharding import PartitionSpec as P
from jax.experimental import pallas as pl
from jax.experimental.pallas import tpu as pltpu

N = 6144


def mirror_pairs(n_recv, n_shot, flip):
    pairs = []
    for i in range(n_recv):
        for j in range(n_shot):
            h = (i % 2) ^ flip
            pairs.append((j * n_recv + i, (i // 2) * n_recv + 2 * j + h))
    return pairs


def gather_line(block):
    n_line = lax.axis_size("zl")
    line_index = lax.axis_index("zl")
    from_left, from_right = [], []
    rightward, leftward = block, block
    for _ in range(n_line - 1):
        rightward = lax.ppermute(rightward, "zl", [(k, k + 1) for k in range(n_line - 1)])
        leftward = lax.ppermute(leftward, "zl", [(k + 1, k) for k in range(n_line - 1)])
        from_left.append(rightward)
        from_right.append(leftward)
    sequence = jnp.stack(from_left[::-1] + [block] + from_right)
    mine = lax.dynamic_slice_in_dim(sequence, n_line - 1 - line_index, n_line, 0)
    other = lax.ppermute(mine, "core", [(0, 1), (1, 0)])
    return mine, other


def product_kernel(left_hbm, panel_hbm, out_ref, lefts, buffers, copied, acc_ref, *, n_block, width, factor):
    chunk_rows = n_block * width
    n_chunks = panel_hbm.shape[2] // chunk_rows
    chunks = [(half, k) for half in range(2) for k in range(n_chunks)]

    def fetch(index):
        half, k = chunks[index]
        return (
            pltpu.make_async_copy(
                panel_hbm.at[half, :, pl.ds(k * chunk_rows, chunk_rows), :],
                buffers.at[index % 2],
                copied.at[0, index % 2],
            ),
            pltpu.make_async_copy(
                left_hbm.at[pl.ds(index * n_block, n_block)], lefts.at[index % 2], copied.at[1, index % 2]
            ),
        )

    for copy in fetch(0):
        copy.start()
    for index, (half, k) in enumerate(chunks):
        if index + 1 < len(chunks):
            for copy in fetch(index + 1):
                copy.start()
        for copy in fetch(index):
            copy.wait()
        for block in range(n_block):
            for p in range(2):
                lhs = lefts[index % 2, block, p, :, :]
                for q in range(2):
                    rhs = buffers[index % 2, q, pl.ds(block * width, width), :]
                    term = jnp.dot(lhs, rhs, preferred_element_type=jnp.float32)
                    if index == 0 and block == 0:
                        acc_ref[p, q] = term
                    else:
                        acc_ref[p, q] += term
    out_ref[0, :, :] = (acc_ref[0, 0] - acc_ref[1, 1]) * factor
    out_ref[1, :, :] = (acc_ref[0, 1] + acc_ref[1, 0]) * factor


def product(left, panels, factor):
    n_blocks, parts, rows, width = left.shape
    cols = panels.shape[-1]
    n_block = n_blocks // 8
    kernel = functools.partial(product_kernel, n_block=n_block, width=width, factor=factor)
    return pl.pallas_call(
        kernel,
        out_shape=jax.ShapeDtypeStruct((2, rows, cols), jnp.float32),
        in_specs=[pl.BlockSpec(memory_space=pl.ANY), pl.BlockSpec(memory_space=pl.ANY)],
        out_specs=pl.BlockSpec(memory_space=pltpu.VMEM),
        scratch_shapes=[
            pltpu.VMEM((2, n_block, parts, rows, width), left.dtype),
            pltpu.VMEM((2, parts, n_block * width, cols), panels.dtype),
            pltpu.SemaphoreType.DMA((2, 2)),
            pltpu.VMEM((2, 2, rows, cols), jnp.float32),
        ],
        cost_estimate=pl.CostEstimate(
            flops=2 * 4 * rows * cols * width * n_blocks,
            transcendentals=0,
            bytes_accessed=2 * (left.size + panels.size) + 4 * 2 * rows * cols,
        ),
    )(left, panels)


def local(pressure):
    n_shot = lax.axis_size("zl") * lax.axis_size("core")
    n_half = lax.axis_size("y") * lax.axis_size("x")
    n_recv = 2 * n_half
    block_rows = pressure.shape[1]
    shot_index = lax.axis_index("zl") * lax.axis_size("core") + lax.axis_index("core")
    half_index = lax.axis_index("zh")
    recv_index = half_index * n_half + lax.axis_index("y") * lax.axis_size("x") + lax.axis_index("x")
    parity = recv_index % 2
    axes = ("zl", "core", "zh", "y", "x")

    arrived = []
    for flip in range(2):
        sent_half = (parity + flip) % 2
        piece = lax.dynamic_slice_in_dim(pressure, sent_half * block_rows, block_rows, 2)
        arrived.append(lax.ppermute(piece, axes, mirror_pairs(n_recv, n_shot, flip)))
    upper = jnp.where(parity == 0, arrived[0], arrived[1])
    lower = jnp.where(parity == 0, arrived[1], arrived[0])
    mirror = jnp.concatenate([upper, lower], axis=1)
    symmetric = (
        (pressure.astype(jnp.float32) + jnp.swapaxes(mirror, 1, 2).astype(jnp.float32)) * 0.5
    ).astype(jnp.bfloat16)

    partner_block = lax.ppermute(symmetric, "zh", [(0, 1), (1, 0)])
    top = jnp.where(half_index == 0, symmetric, partner_block)
    bottom = jnp.where(half_index == 0, partner_block, symmetric)
    panels = lax.all_gather(jnp.stack([top, bottom]), ("y", "x"), axis=2, tiled=True)
    mine, other = gather_line(symmetric)
    core_index = lax.axis_index("core")
    n_line = mine.shape[0]
    natural = jnp.where(
        core_index == 0, jnp.stack([mine, other], axis=1), jnp.stack([other, mine], axis=1)
    ).reshape((2 * n_line,) + symmetric.shape)
    return product(natural, panels, 1.0 / math.sqrt(N))


def solution(mesh):
    n_shot, n_recv = mesh.devices.shape
    n_x = 4
    split = Mesh(
        mesh.devices.reshape(n_shot // 2, 2, 2, n_recv // (2 * n_x), n_x),
        ("zl", "core", "zh", "y", "x"),
    )
    placed = P(None, ("zh", "y", "x"), ("zl", "core"))
    return jax.shard_map(local, mesh=split, in_specs=(placed,), out_specs=placed, check_vma=False)
```
